512 devices in a mesh: grp: 8 (over x, core), dev: 64 (over z, y).
Axes of the slice: x: 4, y: 8, z: 8, core: 2. Of those that a mesh axis runs over, the one named last changes fastest.
Arguments:
- diag_inverse: bfloat16 [1024, 512, 512], P(('grp', 'dev')), may hold values from -1 to 1.5, as said below
- lower_block: bfloat16 [1024, 512, 512], P(('grp', 'dev')), may hold values from -0.15625 to 0.15625
- upper_block: bfloat16 [1024, 512, 512], P(('grp', 'dev')), may hold values from -0.15625 to 0.15625
- right_side: bfloat16 [1024, 512, 128], P(('grp', 'dev')), may hold values from -6 to 6
Outputs:
- solution: bfloat16 [1024, 512, 128], P(('grp', 'dev'))
The draws below stay inside these ranges and needn't reach their ends.
Inputs may be any that keep to these rules, and one draw needn't show every extreme that they name: diag_inverse holds the given inverses of the diagonal blocks.
All inputs are finite; a program needn't handle non-finite values.
Results may differ from the reference program's by a relative error of at most 0.013.
Values may be sent and summed in bfloat16 or wider, within the bound.
A program may use at most 64 MiB of HBM per device.

```python
import math
import jax
import jax.numpy as jnp
from jax import lax

BLOCK = 512
NRHS = 128
NBLOCKS = 1024


def draw_diag_inverse(key, part):
    first_key, second_key = jax.random.split(jax.random.fold_in(key, 17), 2)
    identity = jnp.eye(BLOCK, dtype=jnp.float32)
    offdiag = jnp.clip(jax.random.normal(first_key, (NBLOCKS, BLOCK, BLOCK), jnp.float32), -4.0, 4.0) * (0.4 / math.sqrt(BLOCK))
    diagonal = jax.random.uniform(second_key, (NBLOCKS, BLOCK), jnp.float32, 0.7, 1.3)
    whole = offdiag * (1.0 - identity)[None] + identity[None] * diagonal[:, :, None]
    return whole.astype(jnp.bfloat16)


def shard_levels(key, dims, cuts, least, high):
    level, own = 1.0, jax.random.fold_in(key, 6)
    for dim, shards_of in cuts:
        steps = jnp.exp(jax.random.uniform(jax.random.fold_in(own, dim), (shards_of,), jnp.float32, least / len(cuts), high / len(cuts)))
        level = level * jnp.repeat(steps, dims[dim] // shards_of).reshape([-1 if axis == dim else 1 for axis in range(len(dims))])
    return level


def centred(stream_key, shape, deviation, bound, shards=(), kind=jnp.bfloat16):
    result = jax.random.normal(stream_key, shape, jnp.float32) * deviation
    if len(shards) > 0:
        result = shard_levels(stream_key, shape, shards, -0.22, 0.18) * result
    return jnp.clip(result, min=-bound, max=bound).astype(kind)


def setup_inputs(seed: int = 0) -> dict:
    streams_of = jax.random.split(jax.random.key(seed), 5)
    return {
        "diag_inverse": draw_diag_inverse(jax.random.fold_in(streams_of[4], 71), 0),
        "lower_block": centred(streams_of[1], (NBLOCKS, BLOCK, BLOCK), (3 * BLOCK) ** -0.5, 0.15625, ((0, 512),)),
        "upper_block": centred(streams_of[2], (NBLOCKS, BLOCK, BLOCK), (3 * BLOCK) ** -0.5, 0.15625, ((0, 512),)),
        "right_side": centred(streams_of[3], (NBLOCKS, BLOCK, NRHS), 1.0, 6.0, ((0, 512),)),
    }


def reduce_panel(middle, left_panel, right_panel, order):
    left_spike = middle[:, :order]
    right_spike = middle[:, order:2 * order]
    own_rhs = middle[:, 2 * order:]
    from_left = jnp.dot(left_spike, left_panel, preferred_element_type=jnp.float32)
    from_right = jnp.dot(right_spike, right_panel, preferred_element_type=jnp.float32)
    coupling = from_left[:, order:2 * order] + from_right[:, :order]
    scaling = (jnp.eye(order, dtype=jnp.float32) + coupling).astype(jnp.bfloat16)
    outer_left = from_left[:, :order].astype(jnp.bfloat16)
    outer_right = from_right[:, order:2 * order].astype(jnp.bfloat16)
    remaining = (own_rhs.astype(jnp.float32) - from_left[:, 2 * order:] - from_right[:, 2 * order:]).astype(jnp.bfloat16)
    combined = jnp.concatenate([-outer_left, -outer_right, remaining], axis=1)
    return jnp.dot(scaling, combined, preferred_element_type=jnp.float32).astype(jnp.bfloat16)


def apply_panel(middle, left_values, right_values, order):
    left_spike = middle[:, :order]
    right_spike = middle[:, order:2 * order]
    own_rhs = middle[:, 2 * order:].astype(jnp.float32)
    total = own_rhs - jnp.dot(left_spike, left_values, preferred_element_type=jnp.float32)
    total = total - jnp.dot(right_spike, right_values, preferred_element_type=jnp.float32)
    return total.astype(jnp.bfloat16)


def reduce_level(panels, order):
    count = panels.shape[0]
    zero_row = jnp.zeros((1,) + panels.shape[1:], panels.dtype)
    padded = jnp.concatenate([zero_row, panels, zero_row], axis=0)
    middles = panels[0::2]
    lefts = padded[0:count:2]
    rights = padded[2:count + 2:2]
    return lax.map(lambda items: reduce_panel(items[0], items[1], items[2], order), (middles, lefts, rights))


def reduce_every(panels, order):
    count = panels.shape[0]
    zero_row = jnp.zeros((1,) + panels.shape[1:], panels.dtype)
    padded = jnp.concatenate([zero_row, panels, zero_row], axis=0)
    return lax.map(lambda items: reduce_panel(items[0], items[1], items[2], order), (panels, padded[0:count], padded[2:count + 2]))


def refine(panels, coarse, order):
    zero_row = jnp.zeros((1,) + coarse.shape[1:], coarse.dtype)
    padded = jnp.concatenate([coarse, zero_row], axis=0)
    odd_panels = panels[1::2]
    odd_values = lax.map(lambda items: apply_panel(items[0], items[1], items[2], order), (odd_panels, coarse, padded[1:]))
    return jnp.stack([coarse, odd_values], axis=1).reshape((-1,) + coarse.shape[1:])


def make_panel(items):
    stacked = jnp.concatenate([items[1], items[2], items[3]], axis=1)
    return jnp.dot(items[0], stacked, preferred_element_type=jnp.float32).astype(jnp.bfloat16)


def reference(diag_inverse, lower_block, upper_block, right_side):
    order = BLOCK
    panels = lax.map(make_panel, (diag_inverse, lower_block, upper_block, right_side))
    level_one = reduce_level(panels, order)
    level_two = reduce_every(level_one, order)
    coarse = level_two[:, :, 2 * order:]
    count = coarse.shape[0]
    zero_rows = jnp.zeros((2,) + coarse.shape[1:], coarse.dtype)
    padded = jnp.concatenate([zero_rows, coarse, zero_rows], axis=0)
    top_values = lax.map(lambda items: apply_panel(items[0], items[1], items[2], order), (level_two, padded[0:count], padded[4:count + 4]))
    return refine(panels, top_values, order)
```

```python
import jax
import jax.numpy as jnp
from jax import lax
from jax.experimental import pallas as pl
from jax.experimental.pallas import tpu as pltpu
from jax.sharding import PartitionSpec as P

F32, BF16 = jnp.float32, jnp.bfloat16
MESH = pl.DeviceIdType.MESH
ROWS = ((0, 256), (256, 128), (384, 128))
HALVES = ((0, 256), (256, 256))


def mm(a, b):
    return jnp.dot(a, b, preferred_element_type=F32)


def mv(rows, matrix):
    return lax.dot_general(rows, matrix, (((1,), (1,)), ((), ())), preferred_element_type=F32)


def sweep(groups, slab, diag, lower, upper, right, out, bufs, rhs, zl, zr, fsum, sent, zero, narrow, wide, load, tx, rx):
    n = diag.shape[1]
    total = groups * slab
    me = lax.axis_index("grp") * slab + lax.axis_index("dev")
    has_l, has_r = me > 0, me < total - 1
    at_l, at_r = lax.rem(me + total - 1, total), lax.rem(me + 1, total)
    left = (at_l // slab, lax.rem(at_l, slab))
    right_id = (at_r // slab, lax.rem(at_r, slab))
    (do, uo, lo, de, le, ue) = (bufs.at[i] for i in range(6))
    (A, B, C, E, J, K, CA, T, V, CV, EL, TL, CVL, WR, S, EA, EJ) = (
        bufs.at[i] for i in range(6, 23)
    )
    ro, re = rhs.at[0], rhs.at[1]

    barrier = pltpu.get_barrier_semaphore()

    @pl.when(has_l)
    def _():
        pl.semaphore_signal(barrier, 1, device_id=left, device_id_type=MESH)

    @pl.when(has_r)
    def _():
        pl.semaphore_signal(barrier, 1, device_id=right_id, device_id_type=MESH)

    loads = {}
    order = (
        ("do", diag.at[1], do), ("uo", upper.at[1], uo), ("ro", right.at[1], ro),
        ("lo", lower.at[1], lo), ("de", diag.at[0], de), ("ue", upper.at[0], ue),
        ("le", lower.at[0], le), ("re", right.at[0], re),
    )
    for i, (name, src, dst) in enumerate(order):
        loads[name] = pltpu.make_async_copy(src, dst, load.at[i])
        loads[name].start()

    moves = []

    class Move:
        def __init__(self, src, dst, rightward):
            i = len(moves)
            moves.append(self)
            self.dst, self.sem = dst, rx.at[i]
            self.to, self.come = (has_r, has_l) if rightward else (has_l, has_r)
            self.copy = pltpu.make_async_remote_copy(
                src_ref=src, dst_ref=dst, send_sem=tx.at[i], recv_sem=rx.at[i],
                device_id=right_id if rightward else left, device_id_type=MESH,
            )

        def start(self):
            pl.when(self.to)(self.copy.start)

        def blank(self):
            rows = self.dst.shape[0]
            self.zero = pltpu.make_async_copy(zero.at[pl.ds(0, rows)], self.dst, self.sem)
            pl.when(jnp.logical_not(self.come))(self.zero.start)

        def arrive(self):
            self.copy.wait_recv()

        def drain(self):
            pl.when(self.to)(self.copy.wait_send)

    zero[...] = jnp.zeros_like(zero)

    h, cg, m1, m2 = (sent.at[i] for i in range(4))
    gp, gpp, n1, x = (sent.at[i] for i in range(4, 8))

    def piece(ref, rows):
        return ref.at[pl.ds(rows[0], rows[1])]

    e_moves = [Move(piece(E, r), piece(EL, r), True) for r in ROWS]
    h_move = Move(h, zl.at[0], True)
    t_moves = [Move(piece(T, r), piece(TL, r), False) for r in HALVES]
    cv_moves = [Move(piece(CV, r), piece(CVL, r), True) for r in HALVES]
    cg_move, gp_move = Move(cg, zl.at[1], True), Move(gp, zr.at[0], False)
    m1_move, gpp_move = Move(m1, zl.at[2], True), Move(gpp, zr.at[1], False)
    m2_move, n1_move = Move(m2, zl.at[3], True), Move(n1, zr.at[2], False)
    x_move = Move(x, zr.at[3], False)

    loads["do"].wait()
    loads["uo"].wait()
    for i, r in enumerate(ROWS):
        E[pl.ds(*r), :] = mm(do[pl.ds(*r), :], uo[...]).astype(BF16)
        if i == 0:
            pl.semaphore_wait(barrier, has_l.astype(jnp.int32) + has_r.astype(jnp.int32))
        e_moves[i].start()
        if i == 0:
            for move in moves:
                move.blank()
            loads["ro"].wait()
            h[...] = mv(ro[...].T, do[...]).astype(BF16)
            h_move.start()
    loads["lo"].wait()
    C[...] = mm(do[...], lo[...]).astype(BF16)
    loads["de"].wait()
    loads["ue"].wait()
    B[...] = mm(de[...], ue[...]).astype(BF16)
    loads["le"].wait()
    A[...] = mm(de[...], le[...]).astype(BF16)
    loads["re"].wait()
    g = mv(re[...].T, de[...])
    K[...] = mm(B[...], C[...]).astype(BF16)
    J[...] = mm(B[...], E[...]).astype(BF16)
    CA[...] = mm(C[...], A[...]).astype(BF16)
    fsum[0] = A[...].astype(F32) + mm(K[...], A[...])
    fsum[1] = J[...].astype(F32) + mm(K[...], J[...])
    V[...] = fsum[1].astype(BF16)
    fsum[2] = mm(C[...], V[...])
    q = g - mv(h[...], B[...])
    h_move.arrive()
    q = (q - mv(zl[0], A[...])).astype(BF16)
    qk = q.astype(F32) + mv(q, K[...])

    for i, r in enumerate(ROWS):
        e_moves[i].arrive()
        rows = pl.ds(*r)
        EA[rows, :] = mm(EL[rows, :], A[...]).astype(BF16)
        ta = mm(A[:, rows], EA[rows, :])
        if i < len(ROWS) - 1:
            fsum[0] += ta
        else:
            T[...] = (fsum[0] + ta).astype(BF16)
            t_moves[0].start()
        EJ[rows, :] = mm(EL[rows, :], J[...]).astype(BF16)
        cv = mm(CA[:, rows], EJ[rows, :])
        if i < len(ROWS) - 1:
            fsum[2] += cv
        else:
            CV[...] = (fsum[2] + cv).astype(BF16)
            cv_moves[0].start()
    gpf = qk + mv(mv(q, EL[...]).astype(BF16), A[...])
    gp[...] = gpf.astype(BF16)
    gp_move.start()
    cg[...] = mv(gp[...], C[...]).astype(BF16)
    cg_move.start()
    t_moves[1].start()
    cv_moves[1].start()
    V[...] = (fsum[1] + mm(A[...], EJ[...])).astype(BF16)

    gp_move.arrive()
    cg_move.arrive()
    wide[0] = gp[...].astype(F32) + mv(zl[1], T[...]) + mv(zr[0], V[...])
    r, hold = narrow.at[0], narrow.at[1]
    r[...] = wide[0].astype(BF16)
    for i, rows in enumerate(HALVES):
        t_moves[i].arrive()
        WR[pl.ds(*rows), :] = mm(TL[pl.ds(*rows), :], C[...]).astype(BF16)
    hold[...] = mv(r[...], WR[...]).astype(BF16)
    wide[0] += mv(hold[...], V[...])
    for i in range(len(HALVES)):
        cv_moves[i].arrive()
    hold[...] = mv(r[...], CVL[...]).astype(BF16)
    wide[0] += mv(hold[...], T[...])
    gpp[...] = wide[0].astype(BF16)
    gpp_move.start()
    m1[...] = mv(gpp[...], WR[...]).astype(BF16)
    m1_move.start()
    diagonal = lax.broadcasted_iota(jnp.int32, (n, n), 0) == lax.broadcasted_iota(jnp.int32, (n, n), 1)
    S[...] = (
        jnp.where(diagonal, 1.0, 0.0) + mm(T[...], CVL[...]) + mm(V[...], WR[...])
    ).astype(BF16)
    gpp_move.arrive()
    n1[...] = mv(zr[1], V[...]).astype(BF16)
    n1_move.start()
    m1_move.arrive()
    m2[...] = mv(zl[2], WR[...]).astype(BF16)
    m2_move.start()
    n1_move.arrive()
    w = mv(zr[2], V[...])
    m2_move.arrive()
    w = (w + zl[3].astype(F32)).astype(BF16)
    x[...] = (wide[0] + mv(w, S[...])).astype(BF16)
    x_move.start()
    out[0] = x[...].T
    y = h[...].astype(F32) - mv(x[...], C[...])
    x_move.arrive()
    out[1] = (y - mv(zr[3], E[...])).astype(BF16).T
    for move in moves:
        move.drain()


def body(diag_inverse, lower_block, upper_block, right_side):
    rows, n, nrhs = right_side.shape
    groups, slab = lax.axis_size("grp"), lax.axis_size("dev")

    def kernel(*refs):
        sweep(groups, slab, *refs)

    return pl.pallas_call(
        kernel,
        name="sweep",
        out_shape=jax.ShapeDtypeStruct((rows, n, nrhs), BF16),
        in_specs=[pl.BlockSpec(memory_space=pl.ANY)] * 4,
        out_specs=pl.BlockSpec(memory_space=pltpu.VMEM),
        scratch_shapes=[
            pltpu.VMEM((23, n, n), BF16),
            pltpu.VMEM((rows, n, nrhs), BF16),
            pltpu.VMEM((4, nrhs, n), BF16),
            pltpu.VMEM((4, nrhs, n), BF16),
            pltpu.VMEM((3, n, n), F32),
            pltpu.VMEM((8, nrhs, n), BF16),
            pltpu.VMEM((n // 2, n), BF16),
            pltpu.VMEM((2, nrhs, n), BF16),
            pltpu.VMEM((1, nrhs, n), F32),
            pltpu.SemaphoreType.DMA((8,)),
            pltpu.SemaphoreType.DMA((15,)),
            pltpu.SemaphoreType.DMA((15,)),
        ],
        compiler_params=pltpu.CompilerParams(
            collective_id=0, has_side_effects=True, vmem_limit_bytes=62 * 2**20
        ),
    )(diag_inverse, lower_block, upper_block, right_side)


def solution(mesh):
    spec = P(("grp", "dev"), None, None)
    return jax.shard_map(body, mesh=mesh, in_specs=(spec,) * 4, out_specs=spec, check_vma=False)
```

```python
import jax
import jax.numpy as jnp
from jax import lax
from jax.experimental import pallas as pl
from jax.experimental.pallas import tpu as pltpu
from jax.sharding import PartitionSpec as P

F32, BF16 = jnp.float32, jnp.bfloat16
MESH = pl.DeviceIdType.MESH
ROWS = ((0, 128), (128, 128), (256, 128), (384, 128))
COLUMNS = ((0, 64), (64, 64))
HALVES = ((0, 256), (256, 256))


def mm(a, b):
    return jnp.dot(a, b, preferred_element_type=F32)


def mv(rows, matrix):
    return lax.dot_general(rows, matrix, (((1,), (1,)), ((), ())), preferred_element_type=F32)


def sweep(groups, slab, diag, lower, upper, right, out, bufs, rhs, zl, zr, fsum, sent, zero, narrow, wide, load, tx, rx):
    n = diag.shape[1]
    total = groups * slab
    me = lax.axis_index("grp") * slab + lax.axis_index("dev")
    has_l, has_r = me > 0, me < total - 1
    at_l, at_r = lax.rem(me + total - 1, total), lax.rem(me + 1, total)
    left = (at_l // slab, lax.rem(at_l, slab))
    right_id = (at_r // slab, lax.rem(at_r, slab))
    (do, uo, lo, de, le, ue) = (bufs.at[i] for i in range(6))
    (A, B, C, E, J, K, CA, T, V, CV, EL, TL, CVL, WR, S, EA, EJ) = (
        bufs.at[i] for i in range(6, 23)
    )
    ro, re = rhs.at[0], rhs.at[1]

    barrier = pltpu.get_barrier_semaphore()

    @pl.when(has_l)
    def _():
        pl.semaphore_signal(barrier, 1, device_id=left, device_id_type=MESH)

    loads = {}
    order = (
        ("do", diag.at[1], do), ("uo", upper.at[1], uo), ("ro", right.at[1], ro),
        ("lo", lower.at[1], lo), ("de", diag.at[0], de), ("ue", upper.at[0], ue),
        ("le", lower.at[0], le), ("re", right.at[0], re),
    )
    for i, (name, src, dst) in enumerate(order):
        loads[name] = pltpu.make_async_copy(src, dst, load.at[i])
        if i < 2:
            loads[name].start()

    moves = []

    class Move:
        def __init__(self, src, dst, rightward):
            i = len(moves)
            moves.append(self)
            self.dst, self.sem = dst, rx.at[i]
            self.to, self.come = (has_r, has_l) if rightward else (has_l, has_r)
            self.copy = pltpu.make_async_remote_copy(
                src_ref=src, dst_ref=dst, send_sem=tx.at[i], recv_sem=rx.at[i],
                device_id=right_id if rightward else left, device_id_type=MESH,
            )

        def start(self):
            pl.when(self.to)(self.copy.start)

        def blank(self):
            rows = self.dst.shape[0]
            self.zero = pltpu.make_async_copy(zero.at[pl.ds(0, rows)], self.dst, self.sem)
            pl.when(jnp.logical_not(self.come))(self.zero.start)

        def arrive(self):
            self.copy.wait_recv()

        def drain(self):
            pl.when(self.to)(self.copy.wait_send)

    zero[...] = jnp.zeros_like(zero)

    h, cg, m1, m2 = (sent.at[i] for i in range(4))
    gp, gpp, n1, x = (sent.at[i] for i in range(4, 8))

    def piece(ref, rows):
        return ref.at[pl.ds(rows[0], rows[1])]

    e_moves = [Move(piece(E, r), piece(EL, r), True) for r in ROWS]
    h_move = Move(h, zl.at[0], True)
    t_moves = [Move(piece(T, r), piece(TL, r), False) for r in HALVES]
    cv_moves = [Move(piece(CV, r), piece(CVL, r), True) for r in HALVES]
    cg_move, gp_move = Move(cg, zl.at[1], True), Move(gp, zr.at[0], False)
    m1_moves = [Move(piece(m1, c), piece(zl.at[2], c), True) for c in COLUMNS]
    gpp_moves = [Move(piece(gpp, c), piece(zr.at[1], c), False) for c in COLUMNS]
    m2_moves = [Move(piece(m2, c), piece(zl.at[3], c), True) for c in COLUMNS]
    n1_moves = [Move(piece(n1, c), piece(zr.at[2], c), False) for c in COLUMNS]
    x_moves = [Move(piece(x, c), piece(zr.at[3], c), False) for c in COLUMNS]

    loads["do"].wait()
    loads["uo"].wait()
    for name, _, _ in order[2:]:
        loads[name].start()
    for i, r in enumerate(ROWS):
        E[pl.ds(*r), :] = mm(do[pl.ds(*r), :], uo[...]).astype(BF16)
        if i == 0:
            pl.when(has_r)(lambda: pl.semaphore_wait(barrier, 1))
        e_moves[i].start()
        if i == 0:
            for move in moves:
                move.blank()
    loads["ro"].wait()
    h[...] = mv(ro[...].T, do[...]).astype(BF16)
    h_move.start()
    loads["lo"].wait()
    C[...] = mm(do[...], lo[...]).astype(BF16)
    loads["de"].wait()
    loads["ue"].wait()
    B[...] = mm(de[...], ue[...]).astype(BF16)
    loads["le"].wait()
    A[...] = mm(de[...], le[...]).astype(BF16)
    loads["re"].wait()
    g = mv(re[...].T, de[...])
    K[...] = mm(B[...], C[...]).astype(BF16)
    J[...] = mm(B[...], E[...]).astype(BF16)
    CA[...] = mm(C[...], A[...]).astype(BF16)
    fsum[0] = A[...].astype(F32) + mm(K[...], A[...])
    fsum[1] = J[...].astype(F32) + mm(K[...], J[...])
    V[...] = fsum[1].astype(BF16)
    fsum[2] = mm(C[...], V[...])
    q = g - mv(h[...], B[...])
    wide[0] = q

    for i, r in enumerate(ROWS):
        e_moves[i].arrive()
        rows = pl.ds(*r)
        EA[rows, :] = mm(EL[rows, :], A[...]).astype(BF16)
        ta = mm(A[:, rows], EA[rows, :])
        if i < len(ROWS) - 1:
            fsum[0] += ta
        else:
            T[...] = (fsum[0] + ta).astype(BF16)
            t_moves[0].start()
        EJ[rows, :] = mm(EL[rows, :], J[...]).astype(BF16)
        cv = mm(CA[:, rows], EJ[rows, :])
        if i < len(ROWS) - 1:
            fsum[2] += cv
        else:
            CV[...] = (fsum[2] + cv).astype(BF16)
            cv_moves[0].start()
    r, hold = narrow.at[0], narrow.at[1]
    h_move.arrive()
    wide[0] -= mv(zl[0], A[...])
    r[...] = wide[0].astype(BF16)
    hold[...] = mv(r[...], EL[...]).astype(BF16)
    wide[0] = r[...].astype(F32) + mv(r[...], K[...])
    wide[0] += mv(hold[...], A[...])
    gp[...] = wide[0].astype(BF16)
    gp_move.start()
    cg[...] = mv(gp[...], C[...]).astype(BF16)
    cg_move.start()
    t_moves[1].start()
    cv_moves[1].start()
    V[...] = (fsum[1] + mm(A[...], EJ[...])).astype(BF16)

    gp_move.arrive()
    cg_move.arrive()
    wide[0] = gp[...].astype(F32) + mv(zl[1], T[...]) + mv(zr[0], V[...])
    r[...] = wide[0].astype(BF16)
    for i, rows in enumerate(HALVES):
        t_moves[i].arrive()
        WR[pl.ds(*rows), :] = mm(TL[pl.ds(*rows), :], C[...]).astype(BF16)
    hold[...] = mv(r[...], WR[...]).astype(BF16)
    wide[0] += mv(hold[...], V[...])
    for i in range(len(HALVES)):
        cv_moves[i].arrive()
    hold[...] = mv(r[...], CVL[...]).astype(BF16)
    wide[0] += mv(hold[...], T[...])
    gpp[...] = wide[0].astype(BF16)
    gpp_moves[0].start()
    m1[...] = mv(gpp[...], WR[...]).astype(BF16)
    m1_moves[0].start()
    gpp_moves[1].start()
    m1_moves[1].start()
    diagonal = lax.broadcasted_iota(jnp.int32, (n, n), 0) == lax.broadcasted_iota(jnp.int32, (n, n), 1)
    S[...] = (
        jnp.where(diagonal, 1.0, 0.0) + mm(T[...], CVL[...]) + mm(V[...], WR[...])
    ).astype(BF16)
    for i, c in enumerate(COLUMNS):
        c = pl.ds(*c)
        gpp_moves[i].arrive()
        n1[c, :] = mv(zr[1, c, :], V[...]).astype(BF16)
        n1_moves[i].start()
        m1_moves[i].arrive()
        m2[c, :] = mv(zl[2, c, :], WR[...]).astype(BF16)
        m2_moves[i].start()
    for i, c in enumerate(COLUMNS):
        c = pl.ds(*c)
        n1_moves[i].arrive()
        w = mv(zr[2, c, :], V[...])
        m2_moves[i].arrive()
        hold[c, :] = (w + zl[3, c, :].astype(F32)).astype(BF16)
        x[c, :] = (wide[0, c, :] + mv(hold[c, :], S[...])).astype(BF16)
        x_moves[i].start()
    out[0] = x[...].astype(F32).T
    wide[0] = h[...].astype(F32) - mv(x[...], C[...])
    for i, c in enumerate(COLUMNS):
        c = pl.ds(*c)
        x_moves[i].arrive()
        wide[0, c, :] -= mv(zr[3, c, :], E[...])
    out[1] = wide[0].T
    for move in moves:
        move.drain()


def body(diag_inverse, lower_block, upper_block, right_side):
    rows, n, nrhs = right_side.shape
    groups, slab = lax.axis_size("grp"), lax.axis_size("dev")

    def kernel(*refs):
        sweep(groups, slab, *refs)

    return pl.pallas_call(
        kernel,
        name="sweep",
        out_shape=jax.ShapeDtypeStruct((rows, n, nrhs), F32),
        in_specs=[pl.BlockSpec(memory_space=pl.ANY)] * 4,
        out_specs=pl.BlockSpec(memory_space=pltpu.VMEM),
        scratch_shapes=[
            pltpu.VMEM((23, n, n), BF16),
            pltpu.VMEM((rows, n, nrhs), BF16),
            pltpu.VMEM((4, nrhs, n), BF16),
            pltpu.VMEM((4, nrhs, n), BF16),
            pltpu.VMEM((3, n, n), F32),
            pltpu.VMEM((8, nrhs, n), BF16),
            pltpu.VMEM((n // 2, n), BF16),
            pltpu.VMEM((2, nrhs, n), BF16),
            pltpu.VMEM((1, nrhs, n), F32),
            pltpu.SemaphoreType.DMA((8,)),
            pltpu.SemaphoreType.DMA((21,)),
            pltpu.SemaphoreType.DMA((21,)),
        ],
        compiler_params=pltpu.CompilerParams(
            collective_id=0, has_side_effects=True, vmem_limit_bytes=62 * 2**20
        ),
    )(diag_inverse, lower_block, upper_block, right_side).astype(BF16)


def solution(mesh):
    spec = P(("grp", "dev"), None, None)
    return jax.shard_map(body, mesh=mesh, in_specs=(spec,) * 4, out_specs=spec, check_vma=False)
```

```python
import jax
import jax.numpy as jnp
from jax import lax
from jax.experimental import pallas as pl
from jax.experimental.pallas import tpu as pltpu
from jax.sharding import PartitionSpec as P

F32, BF16 = jnp.float32, jnp.bfloat16
MESH = pl.DeviceIdType.MESH
ROWS = ((0, 128), (128, 128), (256, 128), (384, 128))
COLUMNS = ((0, 64), (64, 64))
HALVES = ((0, 256), (256, 256))


def mm(a, b):
    return jnp.dot(a, b, preferred_element_type=F32)


def mv(rows, matrix):
    return lax.dot_general(rows, matrix, (((1,), (1,)), ((), ())), preferred_element_type=F32)


def sweep(groups, slab, diag, lower, upper, right, out, bufs, rhs, zl, zr, fsum, sent, zero, narrow, wide, load, tx, rx):
    n = diag.shape[1]
    total = groups * slab
    me = lax.axis_index("grp") * slab + lax.axis_index("dev")
    has_l, has_r = me > 0, me < total - 1
    at_l, at_r = lax.rem(me + total - 1, total), lax.rem(me + 1, total)
    left = (at_l // slab, lax.rem(at_l, slab))
    right_id = (at_r // slab, lax.rem(at_r, slab))
    (do, uo, lo, de, le, ue) = (bufs.at[i] for i in range(6))
    (A, B, C, E, J, K, CA, T, V, CV, EL, TL, CVL, WR, S, EA, EJ) = (
        bufs.at[i] for i in range(6, 23)
    )
    ro, re = rhs.at[0], rhs.at[1]

    barrier = pltpu.get_barrier_semaphore()

    @pl.when(has_l)
    def _():
        pl.semaphore_signal(barrier, 1, device_id=left, device_id_type=MESH)

    loads = {}
    order = (
        ("do", diag.at[1], do), ("uo", upper.at[1], uo), ("ro", right.at[1], ro),
        ("lo", lower.at[1], lo), ("de", diag.at[0], de), ("ue", upper.at[0], ue),
        ("le", lower.at[0], le), ("re", right.at[0], re),
    )
    for i, (name, src, dst) in enumerate(order):
        loads[name] = pltpu.make_async_copy(src, dst, load.at[i])
        if i < 2:
            loads[name].start()

    moves = []

    class Move:
        def __init__(self, src, dst, rightward):
            i = len(moves)
            moves.append(self)
            self.dst, self.sem = dst, rx.at[i]
            self.to, self.come = (has_r, has_l) if rightward else (has_l, has_r)
            self.copy = pltpu.make_async_remote_copy(
                src_ref=src, dst_ref=dst, send_sem=tx.at[i], recv_sem=rx.at[i],
                device_id=right_id if rightward else left, device_id_type=MESH,
            )

        def start(self):
            pl.when(self.to)(self.copy.start)

        def blank(self):
            rows = self.dst.shape[0]
            self.zero = pltpu.make_async_copy(zero.at[pl.ds(0, rows)], self.dst, self.sem)
            pl.when(jnp.logical_not(self.come))(self.zero.start)

        def arrive(self):
            self.copy.wait_recv()

        def drain(self):
            pl.when(self.to)(self.copy.wait_send)

    zero[...] = jnp.zeros_like(zero)

    h, cg, m1, m2 = (sent.at[i] for i in range(4))
    gp, gpp, n1, x = (sent.at[i] for i in range(4, 8))

    def piece(ref, rows):
        return ref.at[pl.ds(rows[0], rows[1])]

    e_moves = [Move(piece(E, r), piece(EL, r), True) for r in ROWS]
    h_move = Move(h, zl.at[0], True)
    t_moves = [Move(piece(T, r), piece(TL, r), False) for r in HALVES]
    cv_moves = [Move(piece(CV, r), piece(CVL, r), True) for r in HALVES]
    cg_move, gp_move = Move(cg, zl.at[1], True), Move(gp, zr.at[0], False)
    m1_moves = [Move(piece(m1, c), piece(zl.at[2], c), True) for c in COLUMNS]
    gpp_moves = [Move(piece(gpp, c), piece(zr.at[1], c), False) for c in COLUMNS]
    m2_moves = [Move(piece(m2, c), piece(zl.at[3], c), True) for c in COLUMNS]
    n1_moves = [Move(piece(n1, c), piece(zr.at[2], c), False) for c in COLUMNS]
    x_moves = [Move(piece(x, c), piece(zr.at[3], c), False) for c in COLUMNS]

    loads["do"].wait()
    loads["uo"].wait()
    for name, _, _ in order[2:]:
        loads[name].start()
    for i, r in enumerate(ROWS):
        E[pl.ds(*r), :] = mm(do[pl.ds(*r), :], uo[...]).astype(BF16)
        if i == 0:
            pl.when(has_r)(lambda: pl.semaphore_wait(barrier, 1))
        e_moves[i].start()
        if i == 0:
            for move in moves:
                move.blank()
    loads["ro"].wait()
    h[...] = mv(ro[...].T, do[...]).astype(BF16)
    h_move.start()
    loads["lo"].wait()
    C[...] = mm(do[...], lo[...]).astype(BF16)
    loads["de"].wait()
    loads["ue"].wait()
    B[...] = mm(de[...], ue[...]).astype(BF16)
    loads["le"].wait()
    A[...] = mm(de[...], le[...]).astype(BF16)
    loads["re"].wait()
    g = mv(re[...].T, de[...])
    K[...] = mm(B[...], C[...]).astype(BF16)
    J[...] = mm(B[...], E[...]).astype(BF16)
    CA[...] = mm(C[...], A[...]).astype(BF16)
    fsum[0] = A[...].astype(F32) + mm(K[...], A[...])
    fsum[1] = J[...].astype(F32) + mm(K[...], J[...])
    V[...] = fsum[1].astype(BF16)
    fsum[2] = mm(C[...], V[...])
    q = g - mv(h[...], B[...])
    wide[0] = q

    for i, r in enumerate(ROWS):
        e_moves[i].arrive()
        rows = pl.ds(*r)
        EA[rows, :] = mm(EL[rows, :], A[...]).astype(BF16)
        if i < len(ROWS) - 1:
            fsum[0] += mm(A[:, rows], EA[rows, :])
            EJ[rows, :] = mm(EL[rows, :], J[...]).astype(BF16)
            fsum[2] += mm(CA[:, rows], EJ[rows, :])
    last = pl.ds(*ROWS[-1])
    for i, half in enumerate(HALVES):
        half = pl.ds(*half)
        T[half, :] = (fsum[0, half, :] + mm(A[half, last], EA[last, :])).astype(BF16)
        if i == 0:
            t_moves[0].start()
            EJ[last, :] = mm(EL[last, :], J[...]).astype(BF16)
        CV[half, :] = (fsum[2, half, :] + mm(CA[half, last], EJ[last, :])).astype(BF16)
        if i == 0:
            cv_moves[0].start()
    r, hold = narrow.at[0], narrow.at[1]
    h_move.arrive()
    wide[0] -= mv(zl[0], A[...])
    r[...] = wide[0].astype(BF16)
    hold[...] = mv(r[...], EL[...]).astype(BF16)
    wide[0] = r[...].astype(F32) + mv(r[...], K[...])
    wide[0] += mv(hold[...], A[...])
    gp[...] = wide[0].astype(BF16)
    gp_move.start()
    cg[...] = mv(gp[...], C[...]).astype(BF16)
    cg_move.start()
    t_moves[1].start()
    cv_moves[1].start()
    V[...] = (fsum[1] + mm(A[...], EJ[...])).astype(BF16)

    gp_move.arrive()
    cg_move.arrive()
    wide[0] = gp[...].astype(F32) + mv(zl[1], T[...]) + mv(zr[0], V[...])
    r[...] = wide[0].astype(BF16)
    for i, rows in enumerate(HALVES):
        t_moves[i].arrive()
        WR[pl.ds(*rows), :] = mm(TL[pl.ds(*rows), :], C[...]).astype(BF16)
    hold[...] = mv(r[...], WR[...]).astype(BF16)
    wide[0] += mv(hold[...], V[...])
    for i in range(len(HALVES)):
        cv_moves[i].arrive()
    hold[...] = mv(r[...], CVL[...]).astype(BF16)
    wide[0] += mv(hold[...], T[...])
    gpp[...] = wide[0].astype(BF16)
    gpp_moves[0].start()
    m1[...] = mv(gpp[...], WR[...]).astype(BF16)
    m1_moves[0].start()
    gpp_moves[1].start()
    m1_moves[1].start()
    diagonal = lax.broadcasted_iota(jnp.int32, (n, n), 0) == lax.broadcasted_iota(jnp.int32, (n, n), 1)
    S[...] = (
        jnp.where(diagonal, 1.0, 0.0) + mm(T[...], CVL[...]) + mm(V[...], WR[...])
    ).astype(BF16)
    for i, c in enumerate(COLUMNS):
        c = pl.ds(*c)
        gpp_moves[i].arrive()
        n1[c, :] = mv(zr[1, c, :], V[...]).astype(BF16)
        n1_moves[i].start()
        m1_moves[i].arrive()
        m2[c, :] = mv(zl[2, c, :], WR[...]).astype(BF16)
        m2_moves[i].start()
    for i, c in enumerate(COLUMNS):
        c = pl.ds(*c)
        n1_moves[i].arrive()
        w = mv(zr[2, c, :], V[...])
        m2_moves[i].arrive()
        hold[c, :] = (w + zl[3, c, :].astype(F32)).astype(BF16)
        x[c, :] = (wide[0, c, :] + mv(hold[c, :], S[...])).astype(BF16)
        x_moves[i].start()
    out[0] = x[...].T
    wide[0] = h[...].astype(F32) - mv(x[...], C[...])
    for i, c in enumerate(COLUMNS):
        c = pl.ds(*c)
        x_moves[i].arrive()
        wide[0, c, :] -= mv(zr[3, c, :], E[...])
    out[1] = wide[0].astype(BF16).T
    for move in moves:
        move.drain()


def store(swept):
    def kernel(source, target, sem):
        copy = pltpu.make_async_copy(source, target, sem)
        copy.start()
        copy.wait()

    return pl.pallas_call(
        kernel,
        name="store",
        out_shape=jax.ShapeDtypeStruct(swept.shape, swept.dtype),
        in_specs=[pl.BlockSpec(memory_space=pltpu.VMEM)],
        out_specs=pl.BlockSpec(memory_space=pltpu.HBM),
        scratch_shapes=[pltpu.SemaphoreType.DMA],
        compiler_params=pltpu.CompilerParams(vmem_limit_bytes=16 * 2**20),
    )(swept)


def body(diag_inverse, lower_block, upper_block, right_side):
    rows, n, nrhs = right_side.shape
    groups, slab = lax.axis_size("grp"), lax.axis_size("dev")

    args = [
        pltpu.with_memory_space_constraint(a, pltpu.HBM)
        for a in (diag_inverse, lower_block, upper_block, right_side)
    ]

    def kernel(*refs):
        sweep(groups, slab, *refs)

    swept = pl.pallas_call(
        kernel,
        name="sweep",
        out_shape=jax.ShapeDtypeStruct((rows, n, nrhs), BF16),
        in_specs=[pl.BlockSpec(memory_space=pltpu.HBM)] * 4,
        out_specs=pl.BlockSpec(memory_space=pltpu.VMEM),
        scratch_shapes=[
            pltpu.VMEM((23, n, n), BF16),
            pltpu.VMEM((rows, n, nrhs), BF16),
            pltpu.VMEM((4, nrhs, n), BF16),
            pltpu.VMEM((4, nrhs, n), BF16),
            pltpu.VMEM((3, n, n), F32),
            pltpu.VMEM((8, nrhs, n), BF16),
            pltpu.VMEM((n // 2, n), BF16),
            pltpu.VMEM((2, nrhs, n), BF16),
            pltpu.VMEM((1, nrhs, n), F32),
            pltpu.SemaphoreType.DMA((8,)),
            pltpu.SemaphoreType.DMA((21,)),
            pltpu.SemaphoreType.DMA((21,)),
        ],
        compiler_params=pltpu.CompilerParams(
            collective_id=0, has_side_effects=True, vmem_limit_bytes=40000000
        ),
    )(*args)
    return store(swept)


def solution(mesh):
    spec = P(("grp", "dev"), None, None)
    return jax.shard_map(body, mesh=mesh, in_specs=(spec,) * 4, out_specs=spec, check_vma=False)
```

```python
import jax
import jax.numpy as jnp
from jax import lax
from jax.experimental import pallas as pl
from jax.experimental.pallas import tpu as pltpu
from jax.sharding import PartitionSpec as P

F32, BF16 = jnp.float32, jnp.bfloat16
MESH = pl.DeviceIdType.MESH
ROWS = ((0, 128), (128, 128), (256, 128), (384, 128))
COLUMNS = ((0, 32), (32, 32), (64, 32), (96, 32))
HALVES = ((0, 256), (256, 256))


def mm(a, b):
    return jnp.dot(a, b, preferred_element_type=F32)


def mv(rows, matrix):
    return lax.dot_general(rows, matrix, (((1,), (1,)), ((), ())), preferred_element_type=F32)


def sweep(groups, slab, diag, lower, upper, right, out, bufs, rhs, zl, zr, fsum, sent, zero, narrow, wide, greet, load, tx, rx):
    n = diag.shape[1]
    total = groups * slab
    me = lax.axis_index("grp") * slab + lax.axis_index("dev")
    has_l, has_r = me > 0, me < total - 1
    at_l, at_r = lax.rem(me + total - 1, total), lax.rem(me + 1, total)
    left = (at_l // slab, lax.rem(at_l, slab))
    right_id = (at_r // slab, lax.rem(at_r, slab))
    (do, uo, lo, de, le, ue) = (bufs.at[i] for i in range(6))
    (A, B, C, E, J, K, CA, T, V, CV, EL, TL, CVL, WR, S, EA, EJ, T0, AL, XL) = (
        bufs.at[i] for i in range(6, 26)
    )
    ro, re = rhs.at[0], rhs.at[1]

    barrier = pltpu.get_barrier_semaphore()

    @pl.when(has_l)
    def _():
        pl.semaphore_signal(barrier, 1, device_id=left, device_id_type=MESH)

    loads = {}
    order = (
        ("do", diag.at[1], do), ("uo", upper.at[1], uo), ("de", diag.at[0], de),
        ("le", lower.at[0], le), ("ro", right.at[1], ro), ("lo", lower.at[1], lo),
        ("ue", upper.at[0], ue), ("re", right.at[0], re),
    )
    for i, (name, src, dst) in enumerate(order):
        loads[name] = pltpu.make_async_copy(src, dst, load.at[i])
        if i < 2:
            loads[name].start()

    moves = []

    class Move:
        def __init__(self, src, dst, rightward):
            i = len(moves)
            moves.append(self)
            self.dst, self.sem = dst, rx.at[i]
            self.to, self.come = (has_r, has_l) if rightward else (has_l, has_r)
            self.copy = pltpu.make_async_remote_copy(
                src_ref=src, dst_ref=dst, send_sem=tx.at[i], recv_sem=rx.at[i],
                device_id=right_id if rightward else left, device_id_type=MESH,
            )

        def start(self):
            pl.when(self.to)(self.copy.start)

        def blank(self):
            rows = self.dst.shape[0]
            self.zero = pltpu.make_async_copy(zero.at[pl.ds(0, rows)], self.dst, self.sem)
            pl.when(jnp.logical_not(self.come))(self.zero.start)

        def arrive(self):
            self.copy.wait_recv()

        def drain(self):
            pl.when(self.to)(self.copy.wait_send)

    zero[...] = jnp.zeros_like(zero)

    h, cg, m1, m2 = (sent.at[i] for i in range(4))
    gp, gpp, n1, x = (sent.at[i] for i in range(4, 8))

    def piece(ref, rows):
        return ref.at[pl.ds(rows[0], rows[1])]

    e_moves = [Move(piece(E, r), piece(EL, r), True) for r in ROWS]
    h_move = Move(h, zl.at[0], True)
    a_moves = [Move(piece(A, r), piece(AL, r), False) for r in HALVES]
    t_moves = [Move(piece(T0, r), piece(TL, r), False) for r in HALVES]
    cv_moves = [Move(piece(CV, r), piece(CVL, r), True) for r in HALVES]
    cg_move, gp_move = Move(cg, zl.at[1], True), Move(gp, zr.at[0], False)
    m1_moves = [Move(piece(m1, c), piece(zl.at[2], c), True) for c in COLUMNS]
    gpp_moves = [Move(piece(gpp, c), piece(zr.at[1], c), False) for c in COLUMNS]
    m2_moves = [Move(piece(m2, c), piece(zl.at[3], c), True) for c in COLUMNS]
    n1_moves = [Move(piece(n1, c), piece(zr.at[2], c), False) for c in COLUMNS]
    x_moves = [Move(piece(x, c), piece(zr.at[3], c), False) for c in COLUMNS]

    loads["do"].wait()
    loads["uo"].wait()
    for name, _, _ in order[2:]:
        loads[name].start()
    for i, r in enumerate(ROWS):
        E[pl.ds(*r), :] = mm(do[pl.ds(*r), :], uo[...]).astype(BF16)
        if i == 0:

            @pl.when(has_r)
            def _():
                pl.semaphore_wait(barrier, 1)
                pl.semaphore_signal(greet, 1, device_id=right_id, device_id_type=MESH)

        e_moves[i].start()
        if i == 0:
            for move in moves:
                move.blank()
    loads["de"].wait()
    loads["le"].wait()
    A[...] = mm(de[...], le[...]).astype(BF16)
    pl.when(has_l)(lambda: pl.semaphore_wait(greet, 1))
    for move in a_moves:
        move.start()
    loads["ro"].wait()
    h[...] = mv(ro[...].T, do[...]).astype(BF16)
    h_move.start()
    loads["lo"].wait()
    C[...] = mm(do[...], lo[...]).astype(BF16)
    loads["ue"].wait()
    B[...] = mm(de[...], ue[...]).astype(BF16)
    K[...] = mm(B[...], C[...]).astype(BF16)
    fsum[0] = A[...].astype(F32) + mm(K[...], A[...])
    T0[...] = fsum[0].astype(BF16)
    for move in t_moves:
        move.start()
    loads["re"].wait()
    J[...] = mm(B[...], E[...]).astype(BF16)
    CA[...] = mm(C[...], A[...]).astype(BF16)
    fsum[1] = J[...].astype(F32) + mm(K[...], J[...])
    V[...] = fsum[1].astype(BF16)
    fsum[2] = mm(C[...], V[...])
    wide[0] = mv(re[...].T, de[...])
    wide[0] -= mv(h[...], B[...])

    for i, rows in enumerate(ROWS):
        rows = pl.ds(*rows)
        e_moves[i].arrive()
        EJ[rows, :] = mm(EL[rows, :], J[...]).astype(BF16)
        if i < len(ROWS) - 1:
            fsum[2] += mm(CA[:, rows], EJ[rows, :])
            EA[rows, :] = mm(EL[rows, :], A[...]).astype(BF16)
            fsum[0] += mm(A[:, rows], EA[rows, :])
    last = pl.ds(*ROWS[-1])
    for i, half in enumerate(HALVES):
        half = pl.ds(*half)
        CV[half, :] = (fsum[2, half, :] + mm(CA[half, last], EJ[last, :])).astype(BF16)
        if i == 0:
            cv_moves[0].start()
    EA[last, :] = mm(EL[last, :], A[...]).astype(BF16)
    T[...] = (fsum[0] + mm(A[:, last], EA[last, :])).astype(BF16)
    r, hold = narrow.at[0], narrow.at[1]
    h_move.arrive()
    wide[0] -= mv(zl[0], A[...])
    r[...] = wide[0].astype(BF16)
    hold[...] = mv(r[...], EL[...]).astype(BF16)
    wide[0] = r[...].astype(F32) + mv(r[...], K[...])
    wide[0] += mv(hold[...], A[...])
    gp[...] = wide[0].astype(BF16)
    gp_move.start()
    cg[...] = mv(gp[...], C[...]).astype(BF16)
    cg_move.start()
    cv_moves[1].start()
    V[...] = (fsum[1] + mm(A[...], EJ[...])).astype(BF16)

    for move in a_moves:
        move.arrive()
    XL[...] = mm(E[...], AL[...]).astype(BF16)
    fsum[0] = mm(AL[...], XL[...])
    for i, half in enumerate(HALVES):
        half = pl.ds(*half)
        t_moves[i].arrive()
        XL[half, :] = (fsum[0, half, :] + TL[half, :].astype(F32)).astype(BF16)
        WR[half, :] = mm(XL[half, :], C[...]).astype(BF16)

    gp_move.arrive()
    cg_move.arrive()
    wide[0] = gp[...].astype(F32) + mv(zl[1], T[...]) + mv(zr[0], V[...])
    r[...] = wide[0].astype(BF16)
    hold[...] = mv(r[...], WR[...]).astype(BF16)
    wide[0] += mv(hold[...], V[...])
    for i in range(len(HALVES)):
        cv_moves[i].arrive()
    hold[...] = mv(r[...], CVL[...]).astype(BF16)
    wide[0] += mv(hold[...], T[...])
    gpp[...] = wide[0].astype(BF16)
    gpp_moves[0].start()
    m1[...] = mv(gpp[...], WR[...]).astype(BF16)
    m1_moves[0].start()
    for i in range(1, len(COLUMNS)):
        gpp_moves[i].start()
        m1_moves[i].start()
    diagonal = lax.broadcasted_iota(jnp.int32, (n, n), 0) == lax.broadcasted_iota(jnp.int32, (n, n), 1)
    S[...] = (
        jnp.where(diagonal, 1.0, 0.0) + mm(T[...], CVL[...]) + mm(V[...], WR[...])
    ).astype(BF16)
    def leftward(i):
        c = pl.ds(*COLUMNS[i])
        gpp_moves[i].arrive()
        n1[c, :] = mv(zr[1, c, :], V[...]).astype(BF16)
        n1_moves[i].start()

    def rightward(i):
        c = pl.ds(*COLUMNS[i])
        m1_moves[i].arrive()
        m2[c, :] = mv(zl[2, c, :], WR[...]).astype(BF16)
        m2_moves[i].start()

    pieces = range(len(COLUMNS))
    spot = lax.rem(me, 8)

    @pl.when(spot == 7)
    def _():
        for i in pieces:
            rightward(i)
        for i in pieces:
            leftward(i)

    @pl.when(spot == 0)
    def _():
        for i in pieces:
            leftward(i)
        for i in pieces:
            rightward(i)

    @pl.when(jnp.logical_and(spot > 0, spot < 7))
    def _():
        for i in pieces:
            leftward(i)
            rightward(i)

    for i, c in enumerate(COLUMNS):
        c = pl.ds(*c)
        n1_moves[i].arrive()
        w = mv(zr[2, c, :], V[...])
        m2_moves[i].arrive()
        hold[c, :] = (w + zl[3, c, :].astype(F32)).astype(BF16)
        x[c, :] = (wide[0, c, :] + mv(hold[c, :], S[...])).astype(BF16)
        x_moves[i].start()
    out[0] = x[...].T
    wide[0] = h[...].astype(F32) - mv(x[...], C[...])
    for i, c in enumerate(COLUMNS):
        c = pl.ds(*c)
        x_moves[i].arrive()
        wide[0, c, :] -= mv(zr[3, c, :], E[...])
    out[1] = wide[0].astype(BF16).T
    for move in moves:
        move.drain()


def store(swept):
    def kernel(source, target, sem):
        copy = pltpu.make_async_copy(source, target, sem)
        copy.start()
        copy.wait()

    return pl.pallas_call(
        kernel,
        name="store",
        out_shape=jax.ShapeDtypeStruct(swept.shape, swept.dtype),
        in_specs=[pl.BlockSpec(memory_space=pltpu.VMEM)],
        out_specs=pl.BlockSpec(memory_space=pltpu.HBM),
        scratch_shapes=[pltpu.SemaphoreType.DMA],
        compiler_params=pltpu.CompilerParams(vmem_limit_bytes=16 * 2**20),
    )(swept)


def body(diag_inverse, lower_block, upper_block, right_side):
    rows, n, nrhs = right_side.shape
    groups, slab = lax.axis_size("grp"), lax.axis_size("dev")

    args = [
        pltpu.with_memory_space_constraint(a, pltpu.HBM)
        for a in (diag_inverse, lower_block, upper_block, right_side)
    ]

    def kernel(*refs):
        sweep(groups, slab, *refs)

    swept = pl.pallas_call(
        kernel,
        name="sweep",
        out_shape=jax.ShapeDtypeStruct((rows, n, nrhs), BF16),
        in_specs=[pl.BlockSpec(memory_space=pltpu.HBM)] * 4,
        out_specs=pl.BlockSpec(memory_space=pltpu.VMEM),
        scratch_shapes=[
            pltpu.VMEM((26, n, n), BF16),
            pltpu.VMEM((rows, n, nrhs), BF16),
            pltpu.VMEM((4, nrhs, n), BF16),
            pltpu.VMEM((4, nrhs, n), BF16),
            pltpu.VMEM((3, n, n), F32),
            pltpu.VMEM((8, nrhs, n), BF16),
            pltpu.VMEM((n // 2, n), BF16),
            pltpu.VMEM((2, nrhs, n), BF16),
            pltpu.VMEM((1, nrhs, n), F32),
            pltpu.SemaphoreType.REGULAR,
            pltpu.SemaphoreType.DMA((8,)),
            pltpu.SemaphoreType.DMA((33,)),
            pltpu.SemaphoreType.DMA((33,)),
        ],
        compiler_params=pltpu.CompilerParams(
            collective_id=0, has_side_effects=True, vmem_limit_bytes=40000000
        ),
    )(*args)
    return store(swept)


def solution(mesh):
    spec = P(("grp", "dev"), None, None)
    return jax.shard_map(body, mesh=mesh, in_specs=(spec,) * 4, out_specs=spec, check_vma=False)
```

```python
import jax
import jax.numpy as jnp
from jax import lax
from jax.experimental import pallas as pl
from jax.experimental.pallas import tpu as pltpu
from jax.sharding import PartitionSpec as P

F32, BF16 = jnp.float32, jnp.bfloat16
MESH = pl.DeviceIdType.MESH
ROWS = ((0, 128), (128, 128), (256, 128), (384, 128))
COLUMNS = ((0, 32), (32, 32), (64, 32), (96, 32))
HALVES = ((0, 256), (256, 256))


def mm(a, b):
    return jnp.dot(a, b, preferred_element_type=F32)


def mv(rows, matrix):
    return lax.dot_general(rows, matrix, (((1,), (1,)), ((), ())), preferred_element_type=F32)


def sweep(groups, slab, diag, lower, upper, right, out, bufs, rhs, zl, zr, fsum, sent, zero, narrow, wide, greet, load, tx, rx):
    n = diag.shape[1]
    total = groups * slab
    me = lax.axis_index("grp") * slab + lax.axis_index("dev")
    has_l, has_r = me > 0, me < total - 1
    at_l, at_r = lax.rem(me + total - 1, total), lax.rem(me + 1, total)
    left = (at_l // slab, lax.rem(at_l, slab))
    right_id = (at_r // slab, lax.rem(at_r, slab))
    (do, uo, lo, de, le, ue) = (bufs.at[i] for i in range(6))
    (A, B, C, E, J, K, CA, T, V, CV, EL, TL, CVL, WR, S, EA, EJ, T0, AL, XL) = (
        bufs.at[i] for i in range(6, 26)
    )
    ro, re = rhs.at[0], rhs.at[1]

    barrier = pltpu.get_barrier_semaphore()

    @pl.when(has_l)
    def _():
        pl.semaphore_signal(barrier, 1, device_id=left, device_id_type=MESH)

    loads = {}
    order = (
        ("do", diag.at[1], do), ("uo", upper.at[1], uo), ("de", diag.at[0], de),
        ("le", lower.at[0], le), ("ro", right.at[1], ro), ("lo", lower.at[1], lo),
        ("ue", upper.at[0], ue), ("re", right.at[0], re),
    )
    for i, (name, src, dst) in enumerate(order):
        loads[name] = pltpu.make_async_copy(src, dst, load.at[i])
        if i < 2:
            loads[name].start()

    moves = []

    class Move:
        def __init__(self, src, dst, rightward):
            i = len(moves)
            moves.append(self)
            self.dst, self.sem = dst, rx.at[i]
            self.to, self.come = (has_r, has_l) if rightward else (has_l, has_r)
            self.copy = pltpu.make_async_remote_copy(
                src_ref=src, dst_ref=dst, send_sem=tx.at[i], recv_sem=rx.at[i],
                device_id=right_id if rightward else left, device_id_type=MESH,
            )

        def start(self):
            pl.when(self.to)(self.copy.start)

        def blank(self):
            rows = self.dst.shape[0]
            self.zero = pltpu.make_async_copy(zero.at[pl.ds(0, rows)], self.dst, self.sem)
            pl.when(jnp.logical_not(self.come))(self.zero.start)

        def arrive(self):
            self.copy.wait_recv()

        def drain(self):
            pl.when(self.to)(self.copy.wait_send)

    zero[...] = jnp.zeros_like(zero)

    h, cg, m1, m2 = (sent.at[i] for i in range(4))
    gp, gpp, n1, x = (sent.at[i] for i in range(4, 8))

    def piece(ref, rows):
        return ref.at[pl.ds(rows[0], rows[1])]

    e_moves = [Move(piece(E, r), piece(EL, r), True) for r in ROWS]
    h_move = Move(h, zl.at[0], True)
    a_moves = [Move(piece(A, r), piece(AL, r), False) for r in HALVES]
    t_moves = [Move(piece(T0, r), piece(TL, r), False) for r in HALVES]
    cv_moves = [Move(piece(CV, r), piece(CVL, r), True) for r in HALVES]
    cg_move, gp_move = Move(cg, zl.at[1], True), Move(gp, zr.at[0], False)
    m1_moves = [Move(piece(m1, c), piece(zl.at[2], c), True) for c in COLUMNS]
    gpp_moves = [Move(piece(gpp, c), piece(zr.at[1], c), False) for c in COLUMNS]
    m2_moves = [Move(piece(m2, c), piece(zl.at[3], c), True) for c in COLUMNS]
    n1_moves = [Move(piece(n1, c), piece(zr.at[2], c), False) for c in COLUMNS]
    x_moves = [Move(piece(x, c), piece(zr.at[3], c), False) for c in COLUMNS]

    loads["do"].wait()
    loads["uo"].wait()
    for name, _, _ in order[2:]:
        loads[name].start()
    for i, r in enumerate(ROWS):
        E[pl.ds(*r), :] = mm(do[pl.ds(*r), :], uo[...]).astype(BF16)
        if i == 0:

            @pl.when(has_r)
            def _():
                pl.semaphore_wait(barrier, 1)
                pl.semaphore_signal(greet, 1, device_id=right_id, device_id_type=MESH)

        e_moves[i].start()
        if i == 0:
            for move in moves:
                move.blank()
    loads["de"].wait()
    loads["le"].wait()
    A[...] = mm(de[...], le[...]).astype(BF16)
    pl.when(has_l)(lambda: pl.semaphore_wait(greet, 1))
    for move in a_moves:
        move.start()
    loads["ro"].wait()
    h[...] = mv(ro[...].T, do[...]).astype(BF16)
    h_move.start()
    loads["lo"].wait()
    C[...] = mm(do[...], lo[...]).astype(BF16)
    loads["ue"].wait()
    B[...] = mm(de[...], ue[...]).astype(BF16)
    K[...] = mm(B[...], C[...]).astype(BF16)
    fsum[0] = A[...].astype(F32) + mm(K[...], A[...])
    T0[...] = fsum[0].astype(BF16)
    for move in t_moves:
        move.start()
    loads["re"].wait()
    J[...] = mm(B[...], E[...]).astype(BF16)
    CA[...] = mm(C[...], A[...]).astype(BF16)
    fsum[1] = J[...].astype(F32) + mm(K[...], J[...])
    V[...] = fsum[1].astype(BF16)
    fsum[2] = mm(C[...], V[...])
    wide[0] = mv(re[...].T, de[...])
    wide[0] -= mv(h[...], B[...])

    for i, rows in enumerate(ROWS):
        rows = pl.ds(*rows)
        e_moves[i].arrive()
        EJ[rows, :] = mm(EL[rows, :], J[...]).astype(BF16)
        if i < len(ROWS) - 1:
            fsum[2] += mm(CA[:, rows], EJ[rows, :])
            EA[rows, :] = mm(EL[rows, :], A[...]).astype(BF16)
            fsum[0] += mm(A[:, rows], EA[rows, :])
    last = pl.ds(*ROWS[-1])
    for i, half in enumerate(HALVES):
        half = pl.ds(*half)
        CV[half, :] = (fsum[2, half, :] + mm(CA[half, last], EJ[last, :])).astype(BF16)
        cv_moves[i].start()
    EA[last, :] = mm(EL[last, :], A[...]).astype(BF16)
    T[...] = (fsum[0] + mm(A[:, last], EA[last, :])).astype(BF16)
    r, hold = narrow.at[0], narrow.at[1]
    h_move.arrive()
    wide[0] -= mv(zl[0], A[...])
    r[...] = wide[0].astype(BF16)
    hold[...] = mv(r[...], EL[...]).astype(BF16)
    wide[0] = r[...].astype(F32) + mv(r[...], K[...])
    wide[0] += mv(hold[...], A[...])
    gp[...] = wide[0].astype(BF16)
    gp_move.start()
    cg[...] = mv(gp[...], C[...]).astype(BF16)
    cg_move.start()
    V[...] = (fsum[1] + mm(A[...], EJ[...])).astype(BF16)

    for move in a_moves:
        move.arrive()
    XL[...] = mm(E[...], AL[...]).astype(BF16)
    fsum[0] = mm(AL[...], XL[...])
    for i, half in enumerate(HALVES):
        half = pl.ds(*half)
        t_moves[i].arrive()
        XL[half, :] = (fsum[0, half, :] + TL[half, :].astype(F32)).astype(BF16)
        WR[half, :] = mm(XL[half, :], C[...]).astype(BF16)

    for move in cv_moves:
        move.arrive()
    diagonal = lax.broadcasted_iota(jnp.int32, (n, n), 0) == lax.broadcasted_iota(jnp.int32, (n, n), 1)
    fsum[0] = jnp.where(diagonal, 1.0, 0.0) + mm(V[...], WR[...])
    S[...] = (fsum[0] + mm(T[...], CVL[...])).astype(BF16)
    gp_move.arrive()
    cg_move.arrive()
    wide[0] = gp[...].astype(F32) + mv(zl[1], T[...]) + mv(zr[0], V[...])
    r[...] = wide[0].astype(BF16)
    wide[0] = mv(r[...], S[...])
    gpp[...] = wide[0].astype(BF16)
    gpp_moves[0].start()
    m1[...] = mv(gpp[...], WR[...]).astype(BF16)
    m1_moves[0].start()
    for i in range(1, len(COLUMNS)):
        gpp_moves[i].start()
        m1_moves[i].start()
    def leftward(i):
        c = pl.ds(*COLUMNS[i])
        gpp_moves[i].arrive()
        n1[c, :] = mv(zr[1, c, :], V[...]).astype(BF16)
        n1_moves[i].start()

    def rightward(i):
        c = pl.ds(*COLUMNS[i])
        m1_moves[i].arrive()
        m2[c, :] = mv(zl[2, c, :], WR[...]).astype(BF16)
        m2_moves[i].start()

    pieces = range(len(COLUMNS))
    spot = lax.rem(me, 8)

    @pl.when(spot == 7)
    def _():
        for i in pieces:
            rightward(i)
        for i in pieces:
            leftward(i)

    @pl.when(spot == 0)
    def _():
        for i in pieces:
            leftward(i)
        for i in pieces:
            rightward(i)

    @pl.when(jnp.logical_and(spot > 0, spot < 7))
    def _():
        for i in pieces:
            leftward(i)
            rightward(i)

    for i, c in enumerate(COLUMNS):
        c = pl.ds(*c)
        n1_moves[i].arrive()
        w = mv(zr[2, c, :], V[...])
        m2_moves[i].arrive()
        hold[c, :] = (w + zl[3, c, :].astype(F32)).astype(BF16)
        x[c, :] = (wide[0, c, :] + mv(hold[c, :], S[...])).astype(BF16)
        x_moves[i].start()
    out[0] = x[...].T
    wide[0] = h[...].astype(F32) - mv(x[...], C[...])
    for i, c in enumerate(COLUMNS):
        c = pl.ds(*c)
        x_moves[i].arrive()
        wide[0, c, :] -= mv(zr[3, c, :], E[...])
    out[1] = wide[0].astype(BF16).T
    for move in moves:
        move.drain()


def store(swept):
    def kernel(source, target, sem):
        copy = pltpu.make_async_copy(source, target, sem)
        copy.start()
        copy.wait()

    return pl.pallas_call(
        kernel,
        name="store",
        out_shape=jax.ShapeDtypeStruct(swept.shape, swept.dtype),
        in_specs=[pl.BlockSpec(memory_space=pltpu.VMEM)],
        out_specs=pl.BlockSpec(memory_space=pltpu.HBM),
        scratch_shapes=[pltpu.SemaphoreType.DMA],
        compiler_params=pltpu.CompilerParams(vmem_limit_bytes=16 * 2**20),
    )(swept)


def body(diag_inverse, lower_block, upper_block, right_side):
    rows, n, nrhs = right_side.shape
    groups, slab = lax.axis_size("grp"), lax.axis_size("dev")

    args = [
        pltpu.with_memory_space_constraint(a, pltpu.HBM)
        for a in (diag_inverse, lower_block, upper_block, right_side)
    ]

    def kernel(*refs):
        sweep(groups, slab, *refs)

    swept = pl.pallas_call(
        kernel,
        name="sweep",
        out_shape=jax.ShapeDtypeStruct((rows, n, nrhs), BF16),
        in_specs=[pl.BlockSpec(memory_space=pltpu.HBM)] * 4,
        out_specs=pl.BlockSpec(memory_space=pltpu.VMEM),
        scratch_shapes=[
            pltpu.VMEM((26, n, n), BF16),
            pltpu.VMEM((rows, n, nrhs), BF16),
            pltpu.VMEM((4, nrhs, n), BF16),
            pltpu.VMEM((4, nrhs, n), BF16),
            pltpu.VMEM((3, n, n), F32),
            pltpu.VMEM((8, nrhs, n), BF16),
            pltpu.VMEM((n // 2, n), BF16),
            pltpu.VMEM((2, nrhs, n), BF16),
            pltpu.VMEM((1, nrhs, n), F32),
            pltpu.SemaphoreType.REGULAR,
            pltpu.SemaphoreType.DMA((8,)),
            pltpu.SemaphoreType.DMA((33,)),
            pltpu.SemaphoreType.DMA((33,)),
        ],
        compiler_params=pltpu.CompilerParams(
            collective_id=0, has_side_effects=True, vmem_limit_bytes=40000000
        ),
    )(*args)
    return store(swept)


def solution(mesh):
    spec = P(("grp", "dev"), None, None)
    return jax.shard_map(body, mesh=mesh, in_specs=(spec,) * 4, out_specs=spec, check_vma=False)
```
